32 devices in a mesh: clips: 2 (over y), tm: 4 (over z), rows: 2 (over x), chan: 2 (over core).
Axes of the slice: x: 2, y: 2, z: 4, core: 2. Of those that a mesh axis runs over, the one named last changes fastest.
Arguments:
- frames: bfloat16 [8, 8, 106, 384], P(('clips', 'tm'), 'rows', None, 'chan'), parts along dimension 0, may hold values from -18 to 18
- gain_attn: float32 [384], replicated, may hold values from 0.1 to 1.9
- w_qkv: bfloat16 [384, 1152], P('chan'), may hold values from -2.14330352 to 2.14330352
- w_out: bfloat16 [384, 384], replicated, may hold values from -3 to 3
- gain_conv: float32 [384], replicated, may hold values from 0.1 to 1.9
- w_conv: bfloat16 [3, 3, 3, 384, 384], P(None, None, None, None, 'chan'), may hold values from -0.0625 to 0.0625
Outputs:
- out: bfloat16 [8, 8, 106, 384], P(('clips', 'tm'), 'rows', None, 'chan'), parts along dimension 0
The draws below stay inside these ranges and needn't reach their ends.
There are 2 independent parts, one for each index of `clips`. The reference program is written for one: setup_inputs(seed, part) draws one part's arguments, and reference() takes and returns one part's arrays. A program takes and returns all parts, laid end to end along the dimension named above; an argument that names none is the same for every part. Nothing has to cross between parts.
All inputs are finite; a program needn't handle non-finite values.
Results may differ from the reference program's by a relative error of at most 0.024.
Values may be sent and summed in bfloat16 or wider, within the bound.
A program may use at most 64 MiB of HBM per device.

```python
import math
import jax
import jax.numpy as jnp
from jax import lax

C = 384
W = 106
H = 8
FRAMES = 4


def draw_frames(key, part):
    keys_list = jax.random.split(key, 3)
    column_scale = jnp.exp(jax.random.uniform(keys_list[0], (C,), jnp.float32, math.log(0.3), math.log(3.0)))
    values = jnp.clip(jax.random.normal(keys_list[2], (FRAMES, H, W, C), jnp.float32), -6.0, 6.0) * column_scale
    return values.astype(jnp.bfloat16)


def draw_w_qkv(key, part):
    keys_list = jax.random.split(key, 1)
    inverse_root = C ** (-0.5)
    base = jnp.clip(jax.random.normal(keys_list[0], (C, 3 * C), jnp.float32), -6.0, 6.0) * inverse_root
    column_factor = jnp.where(jnp.arange(3 * C) < 2 * C, 1.2, 1.0)
    result = base * column_factor
    return result.astype(jnp.bfloat16)


def shard_levels(stream_key, shape, cuts, smallest, high):
    def one(position, parts):
        heights = jax.random.uniform(jax.random.fold_in(jax.random.fold_in(stream_key, 6), position), (parts,), jnp.float32, smallest / len(cuts), high / len(cuts))
        return jnp.repeat(jnp.exp(heights), shape[position] // parts).reshape((-1,) + (1,) * (len(shape) - position - 1))

    level = one(*cuts[0])
    for cut in cuts[1:]:
        level = level * one(*cut)
    return level


def bell_draw(own_key, shape, spread, bound, cuts=(), held_as=jnp.bfloat16):
    drawn = spread * jax.random.normal(own_key, shape, jnp.float32)
    if cuts:
        drawn = drawn * shard_levels(own_key, shape, cuts, -0.22, 0.18)
    return jnp.clip(drawn, -bound, bound).astype(held_as)


def setup_inputs(seed: int = 0, part: int = 0) -> dict:
    seeds = jax.random.split(jax.random.key(seed), 7)
    own_keys = jax.random.split(jax.random.fold_in(seeds[6], part), 7)
    return {
        "frames": draw_frames(jax.random.fold_in(jax.random.fold_in(seeds[6], part), 71), part),
        "gain_attn": jnp.clip(1.0 + 0.18 * jax.random.normal(seeds[1], (C,), jnp.float32), 0.1, 1.9),
        "w_qkv": draw_w_qkv(jax.random.fold_in(seeds[6], 71), part),
        "w_out": bell_draw(seeds[3], (C, C), (4 / C ** 0.5), 3.0),
        "gain_conv": jnp.clip(1.0 + 0.18 * jax.random.normal(seeds[4], (C,), jnp.float32), 0.1, 1.9),
        "w_conv": bell_draw(seeds[5], (3, 3, 3, C, C), (27 * C) ** -0.5, 0.0625, ((4, 2),)),
    }


epsilon = 1e-06

def inv_rms(values):
    return lax.rsqrt(lax.optimization_barrier(jnp.mean(values * values, axis=-1, keepdims=True)) + epsilon)

def reference(frames, gain_attn, w_qkv, w_out, gain_conv, w_conv):
    channels = frames.shape[3]
    frame_rows = frames.shape[1]
    frame_cols = frames.shape[2]
    score_scale = channels ** (-0.5)

    def attend(one_frame):
        flat_x = one_frame.reshape(-1, channels).astype(jnp.float32)
        scaled = (flat_x * gain_attn).astype(jnp.bfloat16)
        projected = jnp.dot(scaled, w_qkv, preferred_element_type=jnp.float32)
        qkv_all = (projected * inv_rms(flat_x)).astype(jnp.bfloat16)
        queries = qkv_all[:, :channels]
        keys_all = qkv_all[:, channels:2 * channels]
        values_all = qkv_all[:, 2 * channels:]
        scores = jnp.dot(queries, keys_all.T, preferred_element_type=jnp.float32) * score_scale
        largest = lax.optimization_barrier(jnp.max(scores, axis=1, keepdims=True))
        exponent = jnp.exp(scores - largest)
        weights = exponent.astype(jnp.bfloat16)
        attended = (jnp.dot(weights, values_all, preferred_element_type=jnp.float32) / lax.optimization_barrier(jnp.sum(exponent, axis=1, keepdims=True))).astype(jnp.bfloat16)
        mixed_rows = (flat_x + jnp.dot(attended, w_out, preferred_element_type=jnp.float32)).astype(jnp.bfloat16)
        mixed_float = mixed_rows.astype(jnp.float32)
        normed = jax.nn.silu(mixed_float * inv_rms(mixed_float) * gain_conv).astype(jnp.bfloat16)
        return normed.reshape(frame_rows, frame_cols, channels)
    hidden_all = lax.map(attend, frames)
    padded = jnp.pad(hidden_all, ((2, 0), (1, 1), (1, 1), (0, 0)))

    def convolve(frame_index):
        window = lax.dynamic_slice_in_dim(padded, frame_index, 3, 0)
        accumulated = jnp.zeros((frame_rows * frame_cols, w_conv.shape[4]), jnp.float32)
        for depth_off in range(3):
            for row_off in range(3):
                for col_off in range(3):
                    patch = window[depth_off, row_off:row_off + frame_rows, col_off:col_off + frame_cols]
                    accumulated = accumulated + jnp.dot(patch.reshape(-1, channels), w_conv[depth_off, row_off, col_off], preferred_element_type=jnp.float32)
        return accumulated.astype(jnp.bfloat16).reshape(frame_rows, frame_cols, -1)
    return lax.map(convolve, jnp.arange(frames.shape[0], dtype=jnp.int32))
```

```python
import functools

import jax
import jax.numpy as jnp
from jax import lax
from jax.experimental import pallas as pl
from jax.experimental.pallas import tpu as pltpu
from jax.sharding import PartitionSpec as P

epsilon = 1e-06
MESH = pl.DeviceIdType.MESH
f32 = jnp.float32
bf16 = jnp.bfloat16
groups = 2


def padded_columns(columns):
    return -(-columns // 16) * 16


def kernel(
    n_rows, n_tm, x_hbm, ga_ref, wq_hbm, wo_hbm, gc_ref, wc_hbm, out_ref,
    xs, wq, wo, wc, xf, qkv, nb, acc1, acc2, s0, s1, r0, r1,
    local_sem, wsem, xsend, xrecv, zsend, zrecv,
):
    band, columns, half = x_hbm.shape[1:]
    channels = 2 * half
    height = band * n_rows
    wide = xf.shape[1]
    q_rows = band + min(n_rows - 1, 2)
    r = lax.axis_index("rows")
    c = lax.axis_index("chan")
    t = lax.axis_index("tm")
    other = 1 - c

    own_x = pltpu.make_async_copy(x_hbm.at[0], xs.at[r, c], local_sem.at[0])
    own_w = pltpu.make_async_copy(wq_hbm, wq.at[c], local_sem.at[1])
    own_wo = pltpu.make_async_copy(wo_hbm, wo, local_sem.at[2])
    own_wc = pltpu.make_async_copy(wc_hbm, wc, local_sem.at[3])
    own_x.start()
    own_w.start()

    barrier = pltpu.get_barrier_semaphore()
    pl.semaphore_signal(barrier, inc=1, device_id={"chan": other}, device_id_type=MESH)
    for k in range(1, n_rows):
        pl.semaphore_signal(
            barrier, inc=1, device_id={"rows": lax.rem(r + k, n_rows)}, device_id_type=MESH
        )

    @pl.when(t > 0)
    def _():
        pl.semaphore_signal(barrier, inc=1, device_id={"tm": t - 1}, device_id_type=MESH)

    @pl.when(t < n_tm - 1)
    def _():
        pl.semaphore_signal(barrier, inc=1, device_id={"tm": t + 1}, device_id_type=MESH)

    own_wo.start()
    own_wc.start()
    xf[...] = jnp.zeros_like(xf)
    zero_row = jnp.zeros((wide, nb.shape[2]), bf16)
    nb[1] = zero_row
    nb[band + 2] = zero_row
    neighbours = jnp.where(t > 0, 1, 0) + jnp.where(t < n_tm - 1, 1, 0) + n_rows
    pl.semaphore_wait(barrier, neighbours)

    to_rows = []
    for k in range(1, n_rows):
        copy = pltpu.make_async_remote_copy(
            src_ref=x_hbm.at[0], dst_ref=xs.at[r, c], send_sem=xsend.at[k], recv_sem=xrecv.at[r, c],
            device_id={"rows": lax.rem(r + k, n_rows)}, device_id_type=MESH,
        )
        copy.start()
        to_rows.append(copy)
    to_core = pltpu.make_async_remote_copy(
        src_ref=x_hbm.at[0], dst_ref=xs.at[r, c], send_sem=xsend.at[0], recv_sem=xrecv.at[r, c],
        device_id={"chan": other}, device_id_type=MESH,
    )
    to_core.start()
    w_core = pltpu.make_async_remote_copy(
        src_ref=wq_hbm, dst_ref=wq.at[c], send_sem=wsem.at[0], recv_sem=wsem.at[1],
        device_id={"chan": other}, device_id_type=MESH,
    )
    w_core.start()

    def project(who):
        for i in range(band):
            row = jnp.concatenate([xs[who, 0, i].astype(f32), xs[who, 1, i].astype(f32)], axis=-1)
            xf[who * band + i, 0:columns, :] = row.astype(bf16)
        x = xf[pl.ds(who * band, band)].reshape(band * wide, channels).astype(f32)
        inverse = lax.rsqrt(jnp.mean(x * x, axis=-1, keepdims=True) + epsilon)
        u = (x * ga_ref[...]).astype(bf16)
        proj = jnp.dot(u, wq[...].reshape(channels, 3 * channels), preferred_element_type=f32)
        qkv[pl.ds(who * band, band)] = (
            (proj * inverse).astype(bf16).reshape(band, wide, 3 * channels)
        )

    def arrival(slot_r, slot_c, core):
        return pltpu.make_async_remote_copy(
            src_ref=xs.at[slot_r, slot_c], dst_ref=xs.at[slot_r, slot_c],
            send_sem=xsend.at[0], recv_sem=xrecv.at[slot_r, slot_c],
            device_id={"chan": core}, device_id_type=MESH,
        )

    own_x.wait()
    own_w.wait()
    arrival(r, other, other).wait_recv()
    w_core.wait_recv()
    project(r)

    forwards = []
    for k in range(1, n_rows):
        who = lax.rem(r + n_rows - k, n_rows)
        arrival(who, c, other).wait_recv()
        forward = pltpu.make_async_remote_copy(
            src_ref=xs.at[who, c], dst_ref=xs.at[who, c], send_sem=xsend.at[n_rows + k],
            recv_sem=xrecv.at[who, c], device_id={"chan": other}, device_id_type=MESH,
        )
        forward.start()
        forwards.append(forward)
    for k in range(1, n_rows):
        who = lax.rem(r + n_rows - k, n_rows)
        arrival(who, other, other).wait_recv()
        project(who)

    own_wo.wait()
    start = jnp.clip(r * band - 1, 0, height - q_rows)
    count = q_rows * wide
    q = qkv[pl.ds(start, q_rows), :, 0:channels].reshape(count, channels)
    keys = qkv[:, :, channels : 2 * channels].reshape(height * wide, channels)
    values = qkv[:, :, 2 * channels :].reshape(height * wide, channels)
    scores = lax.dot_general(
        q, keys, (((1,), (1,)), ((), ())), preferred_element_type=f32
    ) * (channels ** (-0.5))
    column = lax.broadcasted_iota(jnp.int32, (1, height * wide), 1)
    scores = jnp.where(lax.rem(column, wide) < columns, scores, -jnp.inf)
    exponent = jnp.exp(scores - jnp.max(scores, axis=1, keepdims=True))
    total = jnp.sum(exponent, axis=1, keepdims=True)
    weighted = jnp.dot(exponent.astype(bf16), values, preferred_element_type=f32)
    attended = (weighted / total).astype(bf16)
    x = xf[pl.ds(start, q_rows)].reshape(count, channels).astype(f32)
    mixed = (x + jnp.dot(attended, wo[...], preferred_element_type=f32)).astype(bf16).astype(f32)
    inverse = lax.rsqrt(jnp.mean(mixed * mixed, axis=-1, keepdims=True) + epsilon)
    v = mixed * inverse * gc_ref[...]
    normed = v / (1.0 + jnp.exp(-v))
    token = lax.broadcasted_iota(jnp.int32, (count, 1), 0)
    normed = jnp.where(lax.rem(token, wide) < columns, normed, 0.0)
    place = start - r * band + 2
    for e, shift in enumerate((1, 0, count - 1)):
        moved = pltpu.roll(normed, shift, 0) if shift else normed
        nb[pl.ds(place, q_rows), :, e * channels : (e + 1) * channels] = moved.astype(
            bf16
        ).reshape(q_rows, wide, channels)

    own_wc.wait()
    per = band // groups

    def tap(a, g, n):
        result = None
        for b in range(3):
            lhs = nb[1 + b + g * n : 1 + b + g * n + n].reshape(n * wide, 3 * channels)
            term = jnp.dot(lhs, wc[3 * a + b], preferred_element_type=f32)
            result = term if result is None else result + term
        return result

    def z_copy(stage, g):
        source, target = ((s0, r0), (s1, r1))[stage]
        return pltpu.make_async_remote_copy(
            src_ref=source.at[g], dst_ref=target.at[g], send_sem=zsend.at[stage, g],
            recv_sem=zrecv.at[stage, g], device_id={"tm": jnp.minimum(t + 1, n_tm - 1)},
            device_id_type=MESH,
        )

    for g in range(groups):
        s0[g] = tap(0, g, per).astype(bf16)

        @pl.when(t < n_tm - 1)
        def _():
            z_copy(0, g).start()

    for g in range(groups):
        acc1[g] = tap(1, g, per)

    for g in range(groups):
        @pl.when(t > 0)
        def _():
            z_copy(0, g).wait_recv()
            acc1[g] += r0[g].astype(f32)

        s1[g] = acc1[g].astype(bf16)

        @pl.when(t < n_tm - 1)
        def _():
            z_copy(1, g).start()

    for g in range(groups):
        acc2[g] = tap(2, g, per)

    for g in range(groups):
        @pl.when(t > 0)
        def _():
            z_copy(1, g).wait_recv()
            acc2[g] += r1[g].astype(f32)

        for i in range(per):
            out_ref[0, g * per + i] = acc2[g, i * wide : i * wide + columns, :].astype(bf16)

    for copy in to_rows + forwards + [to_core, w_core]:
        copy.wait_send()

    @pl.when(t < n_tm - 1)
    def _():
        for g in range(groups):
            z_copy(0, g).wait_send()
            z_copy(1, g).wait_send()


def per_device(n_rows, n_tm, frames, gain_attn, w_qkv, w_out, gain_conv, w_conv):
    _, band, columns, half = frames.shape
    channels = w_out.shape[0]
    out_half = w_conv.shape[4]
    height = band * n_rows
    wide = padded_columns(columns)
    per = band // groups
    anywhere = pl.BlockSpec(memory_space=pl.ANY)
    vmem = pl.BlockSpec(memory_space=pltpu.VMEM)
    chunk = (groups, per * wide, out_half)
    return pl.pallas_call(
        functools.partial(kernel, n_rows, n_tm),
        out_shape=jax.ShapeDtypeStruct((1, band, columns, out_half), bf16),
        in_specs=[anywhere, vmem, anywhere, anywhere, vmem, anywhere],
        out_specs=vmem,
        scratch_shapes=[
            pltpu.VMEM((n_rows, 2, band, columns, half), bf16),
            pltpu.VMEM((2, half, 3 * channels), bf16),
            pltpu.VMEM((channels, channels), bf16),
            pltpu.VMEM((9, 3 * channels, out_half), bf16),
            pltpu.VMEM((height, wide, channels), bf16),
            pltpu.VMEM((height, wide, 3 * channels), bf16),
            pltpu.VMEM((band + 4, wide, 3 * channels), bf16),
            pltpu.VMEM(chunk, f32),
            pltpu.VMEM(chunk, f32),
            pltpu.VMEM(chunk, bf16),
            pltpu.VMEM(chunk, bf16),
            pltpu.VMEM(chunk, bf16),
            pltpu.VMEM(chunk, bf16),
            pltpu.SemaphoreType.DMA((4,)),
            pltpu.SemaphoreType.DMA((2,)),
            pltpu.SemaphoreType.DMA((2 * n_rows,)),
            pltpu.SemaphoreType.DMA((n_rows, 2)),
            pltpu.SemaphoreType.DMA((2, groups)),
            pltpu.SemaphoreType.DMA((2, groups)),
        ],
        compiler_params=pltpu.CompilerParams(
            collective_id=0, has_side_effects=True, vmem_limit_bytes=48 * 1024 * 1024
        ),
    )(
        frames, gain_attn.reshape(1, channels), w_qkv, w_out, gain_conv.reshape(1, channels),
        w_conv.reshape(9, 3 * channels, out_half),
    )


def solution(mesh):
    in_specs = (
        P(("clips", "tm"), "rows", None, "chan"),
        P(),
        P("chan", None),
        P(),
        P(),
        P(None, None, None, None, "chan"),
    )
    out_specs = P(("clips", "tm"), "rows", None, "chan")
    return jax.shard_map(
        functools.partial(per_device, mesh.shape["rows"], mesh.shape["tm"]),
        mesh=mesh, in_specs=in_specs, out_specs=out_specs, check_vma=False,
    )
```

```python
import functools

import jax
import jax.numpy as jnp
from jax import lax
from jax.experimental import pallas as pl
from jax.experimental.pallas import tpu as pltpu
from jax.sharding import PartitionSpec as P

epsilon = 1e-06
MESH = pl.DeviceIdType.MESH
f32 = jnp.float32
bf16 = jnp.bfloat16
groups = 2


def kernel(
    n_rows, n_tm, x_hbm, ga_ref, wq_hbm, wo_hbm, gc_ref, wc_hbm, out_ref,
    xs, wq, wo, wc, xt, wqt, wot, qt, keys, vt, nb, acc1, acc2, s0, s1, r0, r1,
    local_sem, wsem, xsend, xrecv, zsend, zrecv,
):
    band, half, columns = x_hbm.shape[1:]
    channels = 2 * half
    height = band * n_rows
    wide = xt.shape[2]
    q_rows = band + min(n_rows - 1, 2)
    r = lax.axis_index("rows")
    c = lax.axis_index("chan")
    t = lax.axis_index("tm")
    other = 1 - c

    own_x = pltpu.make_async_copy(x_hbm.at[0], xs.at[r, c], local_sem.at[0])
    own_w = pltpu.make_async_copy(wq_hbm, wq.at[c], local_sem.at[1])
    own_wo = pltpu.make_async_copy(wo_hbm, wo, local_sem.at[2])
    own_wc = pltpu.make_async_copy(wc_hbm, wc, local_sem.at[3])
    own_x.start()
    own_w.start()

    barrier = pltpu.get_barrier_semaphore()
    pl.semaphore_signal(barrier, inc=1, device_id={"chan": other}, device_id_type=MESH)
    for k in range(1, n_rows):
        pl.semaphore_signal(
            barrier, inc=1, device_id={"rows": lax.rem(r + k, n_rows)}, device_id_type=MESH
        )

    @pl.when(t > 0)
    def _():
        pl.semaphore_signal(barrier, inc=1, device_id={"tm": t - 1}, device_id_type=MESH)

    @pl.when(t < n_tm - 1)
    def _():
        pl.semaphore_signal(barrier, inc=1, device_id={"tm": t + 1}, device_id_type=MESH)

    own_wo.start()
    own_wc.start()
    xt[...] = jnp.zeros_like(xt)
    zero_row = jnp.zeros(nb.shape[1:], bf16)
    nb[1] = zero_row
    nb[band + 2] = zero_row
    neighbours = jnp.where(t > 0, 1, 0) + jnp.where(t < n_tm - 1, 1, 0) + n_rows
    pl.semaphore_wait(barrier, neighbours)

    to_rows = []
    for k in range(1, n_rows):
        copy = pltpu.make_async_remote_copy(
            src_ref=x_hbm.at[0], dst_ref=xs.at[r, c], send_sem=xsend.at[k], recv_sem=xrecv.at[r, c],
            device_id={"rows": lax.rem(r + k, n_rows)}, device_id_type=MESH,
        )
        copy.start()
        to_rows.append(copy)
    to_core = pltpu.make_async_remote_copy(
        src_ref=x_hbm.at[0], dst_ref=xs.at[r, c], send_sem=xsend.at[0], recv_sem=xrecv.at[r, c],
        device_id={"chan": other}, device_id_type=MESH,
    )
    to_core.start()
    w_core = pltpu.make_async_remote_copy(
        src_ref=wq_hbm, dst_ref=wq.at[c], send_sem=wsem.at[0], recv_sem=wsem.at[1],
        device_id={"chan": other}, device_id_type=MESH,
    )
    w_core.start()

    def as_column(gain_ref):
        return jnp.transpose(jnp.broadcast_to(gain_ref[...], (wide, channels)))

    ga = as_column(ga_ref)
    gc = as_column(gc_ref)

    def project(who):
        us, inverses = [], []
        for i in range(band):
            row = who * band + i
            xt[row, 0:half, 0:columns] = xs[who, 0, i]
            xt[row, half:channels, 0:columns] = xs[who, 1, i]
            x = xt[row].astype(f32)
            us.append((x * ga).astype(bf16))
            inverses.append(lax.rsqrt(jnp.mean(x * x, axis=0, keepdims=True) + epsilon))
        u = jnp.concatenate(us, axis=1)
        inverse = jnp.concatenate(inverses, axis=1)

        def part(index):
            weights = wqt[index * channels : (index + 1) * channels, :]
            proj = jnp.dot(weights, u, preferred_element_type=f32)
            return (proj * inverse).astype(bf16)

        keys[pl.ds(who, 1)] = jnp.transpose(part(1))[None]
        vt[pl.ds(who, 1)] = part(2)[None]
        q = part(0)
        for i in range(band):
            qt[who * band + i] = q[:, i * wide : (i + 1) * wide]

    def arrival(slot_r, slot_c, core):
        return pltpu.make_async_remote_copy(
            src_ref=xs.at[slot_r, slot_c], dst_ref=xs.at[slot_r, slot_c],
            send_sem=xsend.at[0], recv_sem=xrecv.at[slot_r, slot_c],
            device_id={"chan": core}, device_id_type=MESH,
        )

    own_wo.wait()
    wot[...] = jnp.transpose(wo[...])
    own_x.wait()
    own_w.wait()
    w_core.wait_recv()
    wqt[...] = jnp.transpose(wq[...].reshape(channels, 3 * channels))
    arrival(r, other, other).wait_recv()
    project(r)

    forwards = []
    for k in range(1, n_rows):
        who = lax.rem(r + n_rows - k, n_rows)
        arrival(who, c, other).wait_recv()
        forward = pltpu.make_async_remote_copy(
            src_ref=xs.at[who, c], dst_ref=xs.at[who, c], send_sem=xsend.at[n_rows + k],
            recv_sem=xrecv.at[who, c], device_id={"chan": other}, device_id_type=MESH,
        )
        forward.start()
        forwards.append(forward)
    for k in range(1, n_rows):
        who = lax.rem(r + n_rows - k, n_rows)
        arrival(who, other, other).wait_recv()
        project(who)

    start = jnp.clip(r * band - 1, 0, height - q_rows)
    place = start - r * band + 2
    all_keys = keys[...].reshape(height * wide, channels)
    all_values = jnp.concatenate([vt[k] for k in range(n_rows)], axis=1)
    key_cell = lax.rem(lax.broadcasted_iota(jnp.int32, (height * wide, 1), 0), wide)
    for first in range(0, q_rows, 2):
        members = range(first, min(first + 2, q_rows))
        q = jnp.concatenate([qt[start + l] for l in members], axis=1)
        scores = jnp.dot(all_keys, q, preferred_element_type=f32) * (channels ** (-0.5))
        scores = jnp.where(key_cell < columns, scores, -jnp.inf)
        exponent = jnp.exp(scores - jnp.max(scores, axis=0, keepdims=True))
        total = jnp.sum(exponent, axis=0, keepdims=True)
        weighted = jnp.dot(all_values, exponent.astype(bf16), preferred_element_type=f32)
        attended = (weighted / total).astype(bf16)
        added = jnp.dot(wot[...], attended, preferred_element_type=f32)
        for l in members:
            lanes = slice((l - first) * wide, (l - first + 1) * wide)
            x = xt[start + l].astype(f32)
            mixed = (x + added[:, lanes]).astype(bf16).astype(f32)
            inverse = lax.rsqrt(jnp.mean(mixed * mixed, axis=0, keepdims=True) + epsilon)
            v = mixed * inverse * gc
            normed = v / (1.0 + jnp.exp(-v))
            column = lax.broadcasted_iota(jnp.int32, normed.shape, 1)
            normed = jnp.where(column < columns, normed, 0.0)
            for e, shift in enumerate((1, 0, wide - 1)):
                moved = pltpu.roll(normed, shift, 1) if shift else normed
                nb[place + l, e * channels : (e + 1) * channels, :] = moved.astype(bf16)

    own_wc.wait()
    per = band // groups

    def tap(a, g, n):
        result = None
        for b in range(3):
            lhs = jnp.concatenate([wc[9 * a + 3 * b + e] for e in range(3)], axis=1)
            rhs = jnp.concatenate([nb[1 + b + g * n + i] for i in range(n)], axis=1)
            term = jnp.dot(lhs, rhs, preferred_element_type=f32)
            result = term if result is None else result + term
        return result

    def z_copy(stage, g):
        source, target = ((s0, r0), (s1, r1))[stage]
        return pltpu.make_async_remote_copy(
            src_ref=source.at[g], dst_ref=target.at[g], send_sem=zsend.at[stage, g],
            recv_sem=zrecv.at[stage, g], device_id={"tm": jnp.minimum(t + 1, n_tm - 1)},
            device_id_type=MESH,
        )

    for g in range(groups):
        s0[g] = tap(0, g, per).astype(bf16)

        @pl.when(t < n_tm - 1)
        def _():
            z_copy(0, g).start()

    for g in range(groups):
        acc1[g] = tap(1, g, per)

    for g in range(groups):
        @pl.when(t > 0)
        def _():
            z_copy(0, g).wait_recv()
            acc1[g] += r0[g].astype(f32)

        s1[g] = acc1[g].astype(bf16)

        @pl.when(t < n_tm - 1)
        def _():
            z_copy(1, g).start()

    for g in range(groups):
        acc2[g] = tap(2, g, per)

    for g in range(groups):
        @pl.when(t > 0)
        def _():
            z_copy(1, g).wait_recv()
            acc2[g] += r1[g].astype(f32)

        for i in range(per):
            done = acc2[g, :, i * wide : (i + 1) * wide].astype(bf16)
            out_ref[0, g * per + i] = done[:, 0:columns]

    for copy in to_rows + forwards + [to_core, w_core]:
        copy.wait_send()

    @pl.when(t < n_tm - 1)
    def _():
        for g in range(groups):
            z_copy(0, g).wait_send()
            z_copy(1, g).wait_send()


def per_device(n_rows, n_tm, frames, gain_attn, w_qkv, w_out, gain_conv, w_conv):
    _, band, columns, half = frames.shape
    channels = w_out.shape[0]
    out_half = w_conv.shape[4]
    height = band * n_rows
    wide = -(-columns // 128) * 128
    anywhere = pl.BlockSpec(memory_space=pl.ANY)
    vmem = pl.BlockSpec(memory_space=pltpu.VMEM)
    chunk = (groups, out_half, band // groups * wide)
    result = pl.pallas_call(
        functools.partial(kernel, n_rows, n_tm),
        out_shape=jax.ShapeDtypeStruct((1, band, out_half, columns), bf16),
        in_specs=[anywhere, vmem, anywhere, anywhere, vmem, anywhere],
        out_specs=vmem,
        scratch_shapes=[
            pltpu.VMEM((n_rows, 2, band, half, columns), bf16),
            pltpu.VMEM((2, half, 3 * channels), bf16),
            pltpu.VMEM((channels, channels), bf16),
            pltpu.VMEM((27, out_half, channels), bf16),
            pltpu.VMEM((height, channels, wide), bf16),
            pltpu.VMEM((3 * channels, channels), bf16),
            pltpu.VMEM((channels, channels), bf16),
            pltpu.VMEM((height, channels, wide), bf16),
            pltpu.VMEM((n_rows, band * wide, channels), bf16),
            pltpu.VMEM((n_rows, channels, band * wide), bf16),
            pltpu.VMEM((band + 4, 3 * channels, wide), bf16),
            pltpu.VMEM(chunk, f32),
            pltpu.VMEM(chunk, f32),
            pltpu.VMEM(chunk, bf16),
            pltpu.VMEM(chunk, bf16),
            pltpu.VMEM(chunk, bf16),
            pltpu.VMEM(chunk, bf16),
            pltpu.SemaphoreType.DMA((4,)),
            pltpu.SemaphoreType.DMA((2,)),
            pltpu.SemaphoreType.DMA((2 * n_rows,)),
            pltpu.SemaphoreType.DMA((n_rows, 2)),
            pltpu.SemaphoreType.DMA((2, groups)),
            pltpu.SemaphoreType.DMA((2, groups)),
        ],
        compiler_params=pltpu.CompilerParams(
            collective_id=0, has_side_effects=True, vmem_limit_bytes=56 * 1024 * 1024
        ),
    )(
        frames.swapaxes(2, 3), gain_attn.reshape(1, channels), w_qkv, w_out,
        gain_conv.reshape(1, channels),
        w_conv.swapaxes(3, 4).reshape(27, out_half, channels),
    )
    return result.swapaxes(2, 3)


def solution(mesh):
    in_specs = (
        P(("clips", "tm"), "rows", None, "chan"),
        P(),
        P("chan", None),
        P(),
        P(),
        P(None, None, None, None, "chan"),
    )
    out_specs = P(("clips", "tm"), "rows", None, "chan")
    return jax.shard_map(
        functools.partial(per_device, mesh.shape["rows"], mesh.shape["tm"]),
        mesh=mesh, in_specs=in_specs, out_specs=out_specs, check_vma=False,
    )
```

```python
import functools

import jax
import jax.numpy as jnp
from jax import lax
from jax.experimental import pallas as pl
from jax.experimental.pallas import tpu as pltpu
from jax.sharding import PartitionSpec as P

epsilon = 1e-06
MESH = pl.DeviceIdType.MESH
f32 = jnp.float32
bf16 = jnp.bfloat16
groups = 2


def kernel(
    n_rows, n_tm, x_hbm, ga_ref, wq_hbm, wo_hbm, gc_ref, wc_hbm, out_ref,
    xs, wq, wo, wc, xt, wqt, wot, qt, keys, vt, nb, om, ol, oo, acc1, acc2, s0, s1, r0, r1,
    local_sem, wsem, xsend, xrecv, zsend, zrecv,
):
    band, half, columns = x_hbm.shape[1:]
    channels = 2 * half
    height = band * n_rows
    wide = xt.shape[2]
    start_row = lax.axis_index("rows") * band
    r = lax.axis_index("rows")
    c = lax.axis_index("chan")
    t = lax.axis_index("tm")
    other = 1 - c

    own_x = pltpu.make_async_copy(x_hbm.at[0], xs.at[r, c], local_sem.at[0])
    own_w = pltpu.make_async_copy(wq_hbm, wq.at[c], local_sem.at[1])
    own_wo = pltpu.make_async_copy(wo_hbm, wo, local_sem.at[2])
    own_wc = pltpu.make_async_copy(wc_hbm, wc, local_sem.at[3])
    own_x.start()
    own_w.start()

    barrier = pltpu.get_barrier_semaphore()
    pl.semaphore_signal(barrier, inc=1, device_id={"chan": other}, device_id_type=MESH)
    for k in range(1, n_rows):
        pl.semaphore_signal(
            barrier, inc=1, device_id={"rows": lax.rem(r + k, n_rows)}, device_id_type=MESH
        )

    @pl.when(t > 0)
    def _():
        pl.semaphore_signal(barrier, inc=1, device_id={"tm": t - 1}, device_id_type=MESH)

    @pl.when(t < n_tm - 1)
    def _():
        pl.semaphore_signal(barrier, inc=1, device_id={"tm": t + 1}, device_id_type=MESH)

    own_wo.start()
    own_wc.start()
    xt[...] = jnp.zeros_like(xt)
    zero_row = jnp.zeros(nb.shape[1:], bf16)
    nb[0] = zero_row
    nb[band + 1] = zero_row
    neighbours = jnp.where(t > 0, 1, 0) + jnp.where(t < n_tm - 1, 1, 0) + n_rows
    pl.semaphore_wait(barrier, neighbours)

    sent = []
    for i in range(band):
        for k in range(1, n_rows):
            copy = pltpu.make_async_remote_copy(
                src_ref=x_hbm.at[0, i], dst_ref=xs.at[r, c, i], send_sem=xsend.at[k, i],
                recv_sem=xrecv.at[r, c, i], device_id={"rows": lax.rem(r + k, n_rows)},
                device_id_type=MESH,
            )
            copy.start()
            sent.append(copy)
    w_core = pltpu.make_async_remote_copy(
        src_ref=wq_hbm, dst_ref=wq.at[c], send_sem=wsem.at[0], recv_sem=wsem.at[1],
        device_id={"chan": other}, device_id_type=MESH,
    )
    w_core.start()
    for i in range(band):
        copy = pltpu.make_async_remote_copy(
            src_ref=x_hbm.at[0, i], dst_ref=xs.at[r, c, i], send_sem=xsend.at[0, i],
            recv_sem=xrecv.at[r, c, i], device_id={"chan": other}, device_id_type=MESH,
        )
        copy.start()
        sent.append(copy)

    def as_column(gain_ref):
        return jnp.transpose(jnp.broadcast_to(gain_ref[...][None, :], (wide, channels)))

    ga = as_column(ga_ref)
    gc = as_column(gc_ref)

    def project(who, rows):
        us, inverses = [], []
        for i in rows:
            row = who * band + i
            xt[row, 0:half, 0:columns] = xs[who, 0, i]
            xt[row, half:channels, 0:columns] = xs[who, 1, i]
            x = xt[row].astype(f32)
            us.append((x * ga).astype(bf16))
            inverses.append(lax.rsqrt(jnp.mean(x * x, axis=0, keepdims=True) + epsilon))
        u = jnp.concatenate(us, axis=1)
        inverse = jnp.concatenate(inverses, axis=1)
        lanes = slice(rows[0] * wide, (rows[-1] + 1) * wide)

        def part(index):
            weights = wqt[index * channels : (index + 1) * channels, :]
            proj = jnp.dot(weights, u, preferred_element_type=f32)
            return (proj * inverse).astype(bf16)

        keys[pl.ds(who, 1), lanes, :] = jnp.transpose(part(1))[None]
        vt[pl.ds(who, 1), :, lanes] = part(2)[None]
        q = part(0)
        for n, i in enumerate(rows):
            qt[who * band + i] = q[:, n * wide : (n + 1) * wide]

    key_cell = lax.rem(lax.broadcasted_iota(jnp.int32, (band * wide, 1), 0), wide)

    def fold(q, who, state):
        scores = jnp.dot(keys[who], q, preferred_element_type=f32) * (channels ** (-0.5))
        scores = jnp.where(key_cell < columns, scores, -jnp.inf)
        largest = jnp.max(scores, axis=0, keepdims=True)
        if state is not None:
            largest = jnp.maximum(largest, state[0])
        exponent = jnp.exp(scores - largest)
        total = jnp.sum(exponent, axis=0, keepdims=True)
        weighted = jnp.dot(vt[who], exponent.astype(bf16), preferred_element_type=f32)
        if state is not None:
            factor = jnp.exp(state[0] - largest)
            total = total + state[1] * factor
            weighted = weighted + state[2] * factor
        return largest, total, weighted

    def finish(state, members):
        attended = (state[2] / state[1]).astype(bf16)
        added = jnp.dot(wot[...], attended, preferred_element_type=f32)
        for n, (row, slot, valid) in enumerate(members):
            x = xt[row].astype(f32)
            mixed = (x + added[:, n * wide : (n + 1) * wide]).astype(bf16).astype(f32)
            inverse = lax.rsqrt(jnp.mean(mixed * mixed, axis=0, keepdims=True) + epsilon)
            v = mixed * inverse * gc
            normed = v / (1.0 + jnp.exp(-v))
            column = lax.broadcasted_iota(jnp.int32, normed.shape, 1)
            inside = column < (columns if valid is None else jnp.where(valid, columns, 0))
            normed = jnp.where(inside, normed, 0.0)
            for e, shift in enumerate((1, 0, wide - 1)):
                moved = pltpu.roll(normed, shift, 1) if shift else normed
                nb[slot, e * channels : (e + 1) * channels, :] = moved.astype(bf16)

    def arrive(slot_r, slot_c, i):
        pltpu.make_async_remote_copy(
            src_ref=xs.at[slot_r, slot_c, i], dst_ref=xs.at[slot_r, slot_c, i],
            send_sem=xsend.at[0, i], recv_sem=xrecv.at[slot_r, slot_c, i],
            device_id={"chan": other}, device_id_type=MESH,
        ).wait_recv()

    own_wo.wait()
    wot[...] = jnp.transpose(wo[...])
    own_x.wait()
    own_w.wait()
    w_core.wait_recv()
    wqt[...] = jnp.transpose(wq[...].reshape(channels, 3 * channels))
    for i in range(band):
        arrive(r, other, i)
    project(r, range(band))

    per = band // groups

    def own_queries(g):
        return jnp.concatenate([qt[start_row + g * per + i] for i in range(per)], axis=1)

    def keep(g, state):
        om[g], ol[g], oo[g] = state

    def own_fold(g):
        keep(g, fold(own_queries(g), r, None))

    def pass_on(k, rows):
        who = lax.rem(r + n_rows - k, n_rows)
        for i in rows:
            arrive(who, c, i)
            copy = pltpu.make_async_remote_copy(
                src_ref=xs.at[who, c, i], dst_ref=xs.at[who, c, i],
                send_sem=xsend.at[n_rows + k - 1, i], recv_sem=xrecv.at[who, c, i],
                device_id={"chan": other}, device_id_type=MESH,
            )
            copy.start()
            sent.append(copy)

    for g in range(groups):
        own_fold(g)
        for k in range(1, n_rows):
            pass_on(k, range(g * per, (g + 1) * per))
    for k in range(1, n_rows):
        who = lax.rem(r + n_rows - k, n_rows)
        for g in range(2):
            rows = range(g * band // 2, (g + 1) * band // 2)
            for i in rows:
                arrive(who, other, i)
            project(who, rows)

    def rest(g):
        state = om[g], ol[g], oo[g]
        q = own_queries(g)
        for k in range(1, n_rows):
            state = fold(q, lax.rem(r + n_rows - k, n_rows), state)
        members = [
            (start_row + g * per + i, 1 + g * per + i, None) for i in range(per)
        ]
        finish(state, members)

    if n_rows == 2:
        below = r > 0
        halo = [
            (jnp.where(below, start_row - 1, start_row + band), jnp.where(below, 0, band + 1), None)
        ]
    elif n_rows > 2:
        halo = [
            (jnp.maximum(start_row - 1, 0), 0, r > 0),
            (jnp.minimum(start_row + band, height - 1), band + 1, r < n_rows - 1),
        ]
    else:
        halo = []

    def halo_rows():
        if halo:
            q = jnp.concatenate([qt[row] for row, _, _ in halo], axis=1)
            state = None
            for k in range(n_rows):
                state = fold(q, lax.rem(r + n_rows - k, n_rows), state)
            finish(state, halo)

    def tap(a, g):
        result = None
        for b in range(3):
            lhs = jnp.concatenate([wc[9 * a + 3 * b + e] for e in range(3)], axis=1)
            rhs = jnp.concatenate([nb[b + g * per + i] for i in range(per)], axis=1)
            term = jnp.dot(lhs, rhs, preferred_element_type=f32)
            result = term if result is None else result + term
        return result

    def z_copy(stage, g):
        source, target = ((s0, r0), (s1, r1))[stage]
        return pltpu.make_async_remote_copy(
            src_ref=source.at[g], dst_ref=target.at[g], send_sem=zsend.at[stage, g],
            recv_sem=zrecv.at[stage, g], device_id={"tm": jnp.minimum(t + 1, n_tm - 1)},
            device_id_type=MESH,
        )

    def first_tap(g):
        s0[g] = tap(0, g).astype(bf16)

        @pl.when(t < n_tm - 1)
        def _():
            z_copy(0, g).start()

    lead = r if n_rows == 2 else 0
    order = (lead, 1 - lead)
    for g in range(groups):
        rest(g)
    if n_rows > 2:
        halo_rows()
    own_wc.wait()
    first_tap(order[0])
    if n_rows <= 2:
        halo_rows()
    first_tap(order[1])

    for g in order:
        acc1[g] = tap(1, g)

    for g in order:
        @pl.when(t > 0)
        def _():
            z_copy(0, g).wait_recv()
            acc1[g] += r0[g].astype(f32)

        s1[g] = acc1[g].astype(bf16)

        @pl.when(t < n_tm - 1)
        def _():
            z_copy(1, g).start()

    for g in order:
        acc2[g] = tap(2, g)

    for g in order:
        @pl.when(t > 0)
        def _():
            z_copy(1, g).wait_recv()
            acc2[g] += r1[g].astype(f32)

        for i in range(per):
            done = acc2[g, :, i * wide : (i + 1) * wide].astype(bf16)
            out_ref[0, g * per + i] = done[:, 0:columns]

    for copy in sent + [w_core]:
        copy.wait_send()

    @pl.when(t < n_tm - 1)
    def _():
        for g in range(groups):
            z_copy(0, g).wait_send()
            z_copy(1, g).wait_send()


def per_device(n_rows, n_tm, frames, gain_attn, w_qkv, w_out, gain_conv, w_conv):
    _, band, columns, half = frames.shape
    channels = w_out.shape[0]
    out_half = w_conv.shape[4]
    height = band * n_rows
    wide = -(-columns // 128) * 128
    anywhere = pl.BlockSpec(memory_space=pl.ANY)
    vmem = pl.BlockSpec(memory_space=pltpu.VMEM)
    chunk = (groups, out_half, band // groups * wide)
    result = pl.pallas_call(
        functools.partial(kernel, n_rows, n_tm),
        out_shape=jax.ShapeDtypeStruct((1, band, out_half, columns), bf16),
        in_specs=[anywhere, vmem, anywhere, anywhere, vmem, anywhere],
        out_specs=vmem,
        scratch_shapes=[
            pltpu.VMEM((n_rows, 2, band, half, columns), bf16),
            pltpu.VMEM((2, half, 3 * channels), bf16),
            pltpu.VMEM((channels, channels), bf16),
            pltpu.VMEM((27, out_half, channels), bf16),
            pltpu.VMEM((height, channels, wide), bf16),
            pltpu.VMEM((3 * channels, channels), bf16),
            pltpu.VMEM((channels, channels), bf16),
            pltpu.VMEM((height, channels, wide), bf16),
            pltpu.VMEM((n_rows, band * wide, channels), bf16),
            pltpu.VMEM((n_rows, channels, band * wide), bf16),
            pltpu.VMEM((band + 2, 3 * channels, wide), bf16),
            pltpu.VMEM((groups, 1, band // groups * wide), f32),
            pltpu.VMEM((groups, 1, band // groups * wide), f32),
            pltpu.VMEM((groups, channels, band // groups * wide), f32),
            pltpu.VMEM(chunk, f32),
            pltpu.VMEM(chunk, f32),
            pltpu.VMEM(chunk, bf16),
            pltpu.VMEM(chunk, bf16),
            pltpu.VMEM(chunk, bf16),
            pltpu.VMEM(chunk, bf16),
            pltpu.SemaphoreType.DMA((4,)),
            pltpu.SemaphoreType.DMA((2,)),
            pltpu.SemaphoreType.DMA((2 * n_rows, band)),
            pltpu.SemaphoreType.DMA((n_rows, 2, band)),
            pltpu.SemaphoreType.DMA((2, groups)),
            pltpu.SemaphoreType.DMA((2, groups)),
        ],
        compiler_params=pltpu.CompilerParams(
            collective_id=0, has_side_effects=True, vmem_limit_bytes=56 * 1024 * 1024
        ),
    )(
        frames.swapaxes(2, 3), gain_attn, w_qkv, w_out,
        gain_conv,
        w_conv.swapaxes(3, 4).reshape(27, out_half, channels),
    )
    return result.swapaxes(2, 3)


def solution(mesh):
    in_specs = (
        P(("clips", "tm"), "rows", None, "chan"),
        P(),
        P("chan", None),
        P(),
        P(),
        P(None, None, None, None, "chan"),
    )
    out_specs = P(("clips", "tm"), "rows", None, "chan")
    return jax.shard_map(
        functools.partial(per_device, mesh.shape["rows"], mesh.shape["tm"]),
        mesh=mesh, in_specs=in_specs, out_specs=out_specs, check_vma=False,
    )
```

```python
import functools

import jax
import jax.numpy as jnp
from jax import lax
from jax.experimental import pallas as pl
from jax.experimental.pallas import tpu as pltpu
from jax.sharding import PartitionSpec as P

epsilon = 1e-06
MESH = pl.DeviceIdType.MESH
f32 = jnp.float32
bf16 = jnp.bfloat16
groups = 2


def packs(out_half, columns, wide, per):
    left = per * columns - wide
    return per == 2 and 64 < left < 128 and wide == 128 and out_half % (16 * (wide // (left - 64))) == 0


def pack(value, columns):
    out_half, wide = value.shape[0], value.shape[1] // 2
    taken = wide - columns
    narrow = columns - taken - 64
    pieces = wide // narrow
    step = out_half // pieces
    second = value[:, wide:]
    full = jnp.concatenate([value[:, 0:columns], second[:, 0:taken]], axis=1)
    middle = second[:, taken : taken + 64]
    middle = jnp.concatenate([middle[: out_half // 2], middle[out_half // 2 :]], axis=1)
    last = second[:, taken + 64 : columns]
    last = [last[p * step : (p + 1) * step] for p in range(pieces)]
    last.append(jnp.zeros((step, wide - pieces * narrow), f32))
    return jnp.concatenate([full, middle, jnp.concatenate(last, axis=1)], axis=0).astype(bf16)


def unpack(ref_value, out_half, columns):
    value = ref_value.astype(f32)
    wide = value.shape[1]
    taken = wide - columns
    narrow = columns - taken - 64
    pieces = wide // narrow
    full = value[0:out_half]
    middle = value[out_half : out_half + out_half // 2]
    last = value[out_half + out_half // 2 :]
    pad = jnp.zeros((out_half, taken), f32)
    second = jnp.concatenate(
        [
            full[:, columns:],
            jnp.concatenate([middle[:, 0:64], middle[:, 64:128]], axis=0),
            jnp.concatenate(
                [last[:, p * narrow : (p + 1) * narrow] for p in range(pieces)], axis=0
            ),
            pad,
        ],
        axis=1,
    )
    return jnp.concatenate([full[:, 0:columns], pad, second], axis=1)


def kernel(
    n_rows, n_tm, x_hbm, ga_ref, wq_hbm, wo_hbm, gc_ref, wc_hbm, out_ref,
    xs, wq, wo, wc, xt, wqt, wot, qt, keys, vt, nb, om, ol, oo, acc1, acc2, s0, s1, r0, r1,
    local_sem, wsem, xsend, xrecv, zsend, zrecv,
):
    band, half, columns = x_hbm.shape[1:]
    channels = 2 * half
    height = band * n_rows
    wide = xt.shape[2]
    start_row = lax.axis_index("rows") * band
    r = lax.axis_index("rows")
    c = lax.axis_index("chan")
    t = lax.axis_index("tm")
    other = 1 - c

    own_x = pltpu.make_async_copy(x_hbm.at[0], xs.at[r, c], local_sem.at[0])
    own_w = pltpu.make_async_copy(wq_hbm, wq.at[c], local_sem.at[1])
    own_wo = pltpu.make_async_copy(wo_hbm, wo, local_sem.at[2])
    own_wc = pltpu.make_async_copy(wc_hbm, wc, local_sem.at[3])
    own_x.start()
    own_w.start()

    barrier = pltpu.get_barrier_semaphore()
    pl.semaphore_signal(barrier, inc=1, device_id={"chan": other}, device_id_type=MESH)
    for k in range(1, n_rows):
        pl.semaphore_signal(
            barrier, inc=1, device_id={"rows": lax.rem(r + k, n_rows)}, device_id_type=MESH
        )

    @pl.when(t > 0)
    def _():
        pl.semaphore_signal(barrier, inc=1, device_id={"tm": t - 1}, device_id_type=MESH)

    @pl.when(t < n_tm - 1)
    def _():
        pl.semaphore_signal(barrier, inc=1, device_id={"tm": t + 1}, device_id_type=MESH)

    own_wo.start()
    own_wc.start()
    xt[...] = jnp.zeros_like(xt)
    zero_row = jnp.zeros(nb.shape[1:], bf16)
    nb[0] = zero_row
    nb[band + 1] = zero_row
    neighbours = jnp.where(t > 0, 1, 0) + jnp.where(t < n_tm - 1, 1, 0) + n_rows
    pl.semaphore_wait(barrier, neighbours)

    sent = []
    for i in range(band):
        for k in range(1, n_rows):
            copy = pltpu.make_async_remote_copy(
                src_ref=x_hbm.at[0, i], dst_ref=xs.at[r, c, i], send_sem=xsend.at[k, i],
                recv_sem=xrecv.at[r, c, i], device_id={"rows": lax.rem(r + k, n_rows)},
                device_id_type=MESH,
            )
            copy.start()
            sent.append(copy)
    w_core = pltpu.make_async_remote_copy(
        src_ref=wq_hbm, dst_ref=wq.at[c], send_sem=wsem.at[0], recv_sem=wsem.at[1],
        device_id={"chan": other}, device_id_type=MESH,
    )
    w_core.start()
    for i in range(band):
        copy = pltpu.make_async_remote_copy(
            src_ref=x_hbm.at[0, i], dst_ref=xs.at[r, c, i], send_sem=xsend.at[0, i],
            recv_sem=xrecv.at[r, c, i], device_id={"chan": other}, device_id_type=MESH,
        )
        copy.start()
        sent.append(copy)

    def as_column(gain_ref):
        return jnp.transpose(jnp.broadcast_to(gain_ref[...][None, :], (wide, channels)))

    ga = as_column(ga_ref)
    gc = as_column(gc_ref)

    def project(who, rows):
        us, inverses = [], []
        for i in rows:
            row = who * band + i
            xt[row, 0:half, 0:columns] = xs[who, 0, i]
            xt[row, half:channels, 0:columns] = xs[who, 1, i]
            x = xt[row].astype(f32)
            us.append((x * ga).astype(bf16))
            inverses.append(lax.rsqrt(jnp.mean(x * x, axis=0, keepdims=True) + epsilon))
        u = jnp.concatenate(us, axis=1)
        inverse = jnp.concatenate(inverses, axis=1)
        lanes = slice(rows[0] * wide, (rows[-1] + 1) * wide)

        def part(index):
            weights = wqt[index * channels : (index + 1) * channels, :]
            proj = jnp.dot(weights, u, preferred_element_type=f32)
            return (proj * inverse).astype(bf16)

        keys[pl.ds(who, 1), lanes, :] = jnp.transpose(part(1))[None]
        vt[pl.ds(who, 1), :, lanes] = part(2)[None]
        q = part(0)
        for n, i in enumerate(rows):
            qt[who * band + i] = q[:, n * wide : (n + 1) * wide]

    key_cell = lax.rem(lax.broadcasted_iota(jnp.int32, (band * wide, 1), 0), wide)

    def fold(q, who, state):
        scores = jnp.dot(keys[who], q, preferred_element_type=f32) * (channels ** (-0.5))
        scores = jnp.where(key_cell < columns, scores, -jnp.inf)
        largest = jnp.max(scores, axis=0, keepdims=True)
        if state is not None:
            largest = jnp.maximum(largest, state[0])
        exponent = jnp.exp(scores - largest)
        total = jnp.sum(exponent, axis=0, keepdims=True)
        weighted = jnp.dot(vt[who], exponent.astype(bf16), preferred_element_type=f32)
        if state is not None:
            factor = jnp.exp(state[0] - largest)
            total = total + state[1] * factor
            weighted = weighted + state[2] * factor
        return largest, total, weighted

    def finish(state, members):
        attended = (state[2] / state[1]).astype(bf16)
        added = jnp.dot(wot[...], attended, preferred_element_type=f32)
        for n, (row, slot, valid) in enumerate(members):
            x = xt[row].astype(f32)
            mixed = (x + added[:, n * wide : (n + 1) * wide]).astype(bf16).astype(f32)
            inverse = lax.rsqrt(jnp.mean(mixed * mixed, axis=0, keepdims=True) + epsilon)
            v = mixed * inverse * gc
            normed = v / (1.0 + jnp.exp(-v))
            column = lax.broadcasted_iota(jnp.int32, normed.shape, 1)
            inside = column < (columns if valid is None else jnp.where(valid, columns, 0))
            normed = jnp.where(inside, normed, 0.0)
            for e, shift in enumerate((1, 0, wide - 1)):
                moved = pltpu.roll(normed, shift, 1) if shift else normed
                nb[slot, e * channels : (e + 1) * channels, :] = moved.astype(bf16)

    def arrive(slot_r, slot_c, i):
        pltpu.make_async_remote_copy(
            src_ref=xs.at[slot_r, slot_c, i], dst_ref=xs.at[slot_r, slot_c, i],
            send_sem=xsend.at[0, i], recv_sem=xrecv.at[slot_r, slot_c, i],
            device_id={"chan": other}, device_id_type=MESH,
        ).wait_recv()

    own_wo.wait()
    wot[...] = jnp.transpose(wo[...])
    own_x.wait()
    own_w.wait()
    w_core.wait_recv()
    wqt[...] = jnp.transpose(wq[...].reshape(channels, 3 * channels))
    for i in range(band):
        arrive(r, other, i)
    project(r, range(band))

    per = band // groups

    def own_queries(g):
        return jnp.concatenate([qt[start_row + g * per + i] for i in range(per)], axis=1)

    def keep(g, state):
        om[g], ol[g], oo[g] = state

    def own_fold(g):
        keep(g, fold(own_queries(g), r, None))

    def pass_on(k, rows):
        who = lax.rem(r + n_rows - k, n_rows)
        for i in rows:
            arrive(who, c, i)
            copy = pltpu.make_async_remote_copy(
                src_ref=xs.at[who, c, i], dst_ref=xs.at[who, c, i],
                send_sem=xsend.at[n_rows + k - 1, i], recv_sem=xrecv.at[who, c, i],
                device_id={"chan": other}, device_id_type=MESH,
            )
            copy.start()
            sent.append(copy)

    for g in range(groups):
        own_fold(g)
        for k in range(1, n_rows):
            pass_on(k, range(g * per, (g + 1) * per))
    for k in range(1, n_rows):
        who = lax.rem(r + n_rows - k, n_rows)
        for g in range(2):
            rows = range(g * band // 2, (g + 1) * band // 2)
            for i in rows:
                arrive(who, other, i)
            project(who, rows)

    def rest(g):
        state = om[g], ol[g], oo[g]
        q = own_queries(g)
        for k in range(1, n_rows):
            state = fold(q, lax.rem(r + n_rows - k, n_rows), state)
        members = [
            (start_row + g * per + i, 1 + g * per + i, None) for i in range(per)
        ]
        finish(state, members)

    if n_rows == 2:
        below = r > 0
        halo = [
            (jnp.where(below, start_row - 1, start_row + band), jnp.where(below, 0, band + 1), None)
        ]
    elif n_rows > 2:
        halo = [
            (jnp.maximum(start_row - 1, 0), 0, r > 0),
            (jnp.minimum(start_row + band, height - 1), band + 1, r < n_rows - 1),
        ]
    else:
        halo = []

    def halo_rows():
        if halo:
            q = jnp.concatenate([qt[row] for row, _, _ in halo], axis=1)
            state = None
            for k in range(n_rows):
                state = fold(q, lax.rem(r + n_rows - k, n_rows), state)
            finish(state, halo)

    def tap(a, g):
        result = None
        for b in range(3):
            lhs = jnp.concatenate([wc[9 * a + 3 * b + e] for e in range(3)], axis=1)
            rhs = jnp.concatenate([nb[b + g * per + i] for i in range(per)], axis=1)
            term = jnp.dot(lhs, rhs, preferred_element_type=f32)
            result = term if result is None else result + term
        return result

    def z_copy(stage, g):
        source, target = ((s0, r0), (s1, r1))[stage]
        return pltpu.make_async_remote_copy(
            src_ref=source.at[g], dst_ref=target.at[g], send_sem=zsend.at[stage, g],
            recv_sem=zrecv.at[stage, g], device_id={"tm": jnp.minimum(t + 1, n_tm - 1)},
            device_id_type=MESH,
        )

    packed = packs(half, columns, wide, per)

    def pressed(value):
        return pack(value, columns) if packed else value.astype(bf16)

    def spread(value):
        return unpack(value, half, columns) if packed else value.astype(f32)

    def first_tap(g):
        s0[g] = pressed(tap(0, g))

        @pl.when(t < n_tm - 1)
        def _():
            z_copy(0, g).start()

    lead = r if n_rows == 2 else 0
    order = (lead, 1 - lead)
    for g in range(groups):
        rest(g)
    if n_rows > 2:
        halo_rows()
    own_wc.wait()
    first_tap(order[0])
    if n_rows <= 2:
        halo_rows()
    first_tap(order[1])

    for g in order:
        acc1[g] = tap(1, g)

    for g in order:
        @pl.when(t > 0)
        def _():
            z_copy(0, g).wait_recv()
            acc1[g] += spread(r0[g])

        s1[g] = pressed(acc1[g])

        @pl.when(t < n_tm - 1)
        def _():
            z_copy(1, g).start()

    for g in order:
        acc2[g] = tap(2, g)

    for g in order:
        @pl.when(t > 0)
        def _():
            z_copy(1, g).wait_recv()
            acc2[g] += spread(r1[g])

        for i in range(per):
            done = acc2[g, :, i * wide : (i + 1) * wide].astype(bf16)
            out_ref[0, g * per + i] = done[:, 0:columns]

    for copy in sent + [w_core]:
        copy.wait_send()

    @pl.when(t < n_tm - 1)
    def _():
        for g in range(groups):
            z_copy(0, g).wait_send()
            z_copy(1, g).wait_send()


def per_device(n_rows, n_tm, frames, gain_attn, w_qkv, w_out, gain_conv, w_conv):
    _, band, columns, half = frames.shape
    channels = w_out.shape[0]
    out_half = w_conv.shape[4]
    height = band * n_rows
    wide = -(-columns // 128) * 128
    anywhere = pl.BlockSpec(memory_space=pl.ANY)
    vmem = pl.BlockSpec(memory_space=pltpu.VMEM)
    chunk = (groups, out_half, band // groups * wide)
    travel = chunk
    if packs(out_half, columns, wide, band // groups):
        left = (band // groups) * columns - wide - 64
        travel = (groups, out_half + out_half // 2 + out_half // (wide // left), wide)
    result = pl.pallas_call(
        functools.partial(kernel, n_rows, n_tm),
        out_shape=jax.ShapeDtypeStruct((1, band, out_half, columns), bf16),
        in_specs=[anywhere, vmem, anywhere, anywhere, vmem, anywhere],
        out_specs=vmem,
        scratch_shapes=[
            pltpu.VMEM((n_rows, 2, band, half, columns), bf16),
            pltpu.VMEM((2, half, 3 * channels), bf16),
            pltpu.VMEM((channels, channels), bf16),
            pltpu.VMEM((27, out_half, channels), bf16),
            pltpu.VMEM((height, channels, wide), bf16),
            pltpu.VMEM((3 * channels, channels), bf16),
            pltpu.VMEM((channels, channels), bf16),
            pltpu.VMEM((height, channels, wide), bf16),
            pltpu.VMEM((n_rows, band * wide, channels), bf16),
            pltpu.VMEM((n_rows, channels, band * wide), bf16),
            pltpu.VMEM((band + 2, 3 * channels, wide), bf16),
            pltpu.VMEM((groups, 1, band // groups * wide), f32),
            pltpu.VMEM((groups, 1, band // groups * wide), f32),
            pltpu.VMEM((groups, channels, band // groups * wide), f32),
            pltpu.VMEM(chunk, f32),
            pltpu.VMEM(chunk, f32),
            pltpu.VMEM(travel, bf16),
            pltpu.VMEM(travel, bf16),
            pltpu.VMEM(travel, bf16),
            pltpu.VMEM(travel, bf16),
            pltpu.SemaphoreType.DMA((4,)),
            pltpu.SemaphoreType.DMA((2,)),
            pltpu.SemaphoreType.DMA((2 * n_rows, band)),
            pltpu.SemaphoreType.DMA((n_rows, 2, band)),
            pltpu.SemaphoreType.DMA((2, groups)),
            pltpu.SemaphoreType.DMA((2, groups)),
        ],
        compiler_params=pltpu.CompilerParams(
            collective_id=0, has_side_effects=True, vmem_limit_bytes=56 * 1024 * 1024
        ),
    )(
        frames.swapaxes(2, 3), gain_attn, w_qkv, w_out,
        gain_conv,
        w_conv.swapaxes(3, 4).reshape(27, out_half, channels),
    )
    return result.swapaxes(2, 3)


def solution(mesh):
    in_specs = (
        P(("clips", "tm"), "rows", None, "chan"),
        P(),
        P("chan", None),
        P(),
        P(),
        P(None, None, None, None, "chan"),
    )
    out_specs = P(("clips", "tm"), "rows", None, "chan")
    return jax.shard_map(
        functools.partial(per_device, mesh.shape["rows"], mesh.shape["tm"]),
        mesh=mesh, in_specs=in_specs, out_specs=out_specs, check_vma=False,
    )
```
